128 devices in a mesh: band: 16 (over z, x), rows: 8 (over y, core).
Axes of the slice: x: 4, y: 4, z: 4, core: 2. Of those that a mesh axis runs over, the one named last changes fastest.
Arguments:
- latents: bfloat16 [107520, 16], P(('band', 'rows')), may hold values from -6 to 6
- token_cell: int32 [107520], P(('band', 'rows')), may hold values from 0 to 107519, as said below
- frame_counts: int32 [16], replicated, may hold values from 1 to 4, 21 in all
- in_kernel: bfloat16 [3, 3, 3, 16, 384], replicated, may hold values from -0.3125 to 0.3125
- in_bias: float32 [384], replicated, may hold values from -3 to 3
- mid_kernel: bfloat16 [3, 3, 3, 384, 384], replicated, may hold values from -0.0625 to 0.0625
- mid_bias: float32 [384], replicated, may hold values from -3 to 3
Outputs:
- decoded: bfloat16 [64, 32, 160, 384], P('band', 'rows')
The draws below stay inside these ranges and needn't reach their ends.
Inputs may be any that keep to these rules, and one draw needn't show every extreme that they name: `token_cell`: rows d * 840 to (d + 1) * 840 - 1 (d the flat index over band+rows) are, in some order, the cells f * 32 * 160 + d * 40 + s for every f < 21 and s < 40, each once. `frame_counts`: the counts sum to 21; some band holds 4 frames.
All inputs are finite; a program needn't handle non-finite values.
Results may differ from the reference program's by a relative error of at most 0.0043.
Values may be sent and summed in bfloat16 or wider, within the bound.
No kernel may reach another device: no remote copies, remote signals or barrier semaphores. Data moves between devices by JAX's collectives and lax.ppermute only.
A program may use at most 64 MiB of HBM per device.

```python
import math
import jax
import jax.numpy as jnp
import numpy as np
from jax import lax

Z = 16
C = 384
W = 160
FCAP = 4
FRAMES = 21
H = 32
SPAN = 40
TOK_DEV = 840
TOKENS = 107520
N_BAND = 16


def draw_token_cell(key, part):
    devices = TOKENS // TOK_DEV
    subkeys = jax.random.split(key, devices)

    def shuffle(subkey):
        return jax.random.permutation(subkey, TOK_DEV)
    local_order = jax.vmap(shuffle)(subkeys).astype(jnp.int32)
    device_ids = jnp.arange(devices, dtype=jnp.int32)[:, None]
    cells = local_order // SPAN * (H * W) + device_ids * SPAN + local_order % SPAN
    return cells.reshape(-1).astype(jnp.int32)


def levels(key, shape, cuts, smallest, high):
    level, own = 1.0, jax.random.fold_in(key, 6)
    for dim, shards_of in cuts:
        steps = jnp.exp(jax.random.uniform(jax.random.fold_in(own, dim), (shards_of,), jnp.float32, smallest / len(cuts), high / len(cuts)))
        level = level * jnp.repeat(steps, shape[dim] // shards_of).reshape([-1 if axis == dim else 1 for axis in range(len(shape))])
    return level


def split_up(number_of, total, bound, lean):
    weights = [(1 << 20) // math.isqrt(rank ** lean) + 1 for rank in range(2, number_of + 1)]
    surplus, holding = total - bound - (number_of - 1), [1] * (number_of - 1)
    while surplus > 0:
        candidates = [i for i in range(number_of - 1) if holding[i] < bound]
        mass, remaining = sum([weights[i] for i in candidates]), surplus
        for i in candidates:
            extra = min(bound - holding[i], max(1, remaining * weights[i] // mass), surplus)
            holding[i] = holding[i] + extra
            surplus = surplus - extra
    return np.array([bound] + holding)


def ragged(stream_key, amount, total, bound, skew):
    if amount == 2:
        one = jax.random.randint(stream_key, (), max(1, total - bound), min(bound, total - 1) + 1)
        return jnp.stack([one, total - one])
    sizes = jnp.asarray(split_up(amount, total, bound, skew), jnp.int32)
    couples = (amount - 1) // 2
    source_of, sink = sizes[1:1 + 2 * couples:2], sizes[2:2 + 2 * couples:2]
    slack = jnp.minimum(source_of - 1, bound - sink)
    moved = jax.random.randint(jax.random.fold_in(stream_key, 1), (couples,), 0, 1 << 20) % (slack + 1)
    sizes = sizes.at[1:1 + 2 * couples:2].set(source_of - moved).at[2:2 + 2 * couples:2].set(sink + moved)
    return sizes[jax.random.permutation(jax.random.fold_in(stream_key, 2), amount)]


def noise(rng, shape, deviation, limit, cuts=(), kind=jnp.bfloat16):
    gain = levels(rng, shape, cuts, -0.22, 0.18) if cuts else 1.0
    values = jax.random.normal(rng, shape, jnp.float32) * deviation * gain
    return jnp.minimum(jnp.maximum(values, -limit), limit).astype(kind)


def setup_inputs(seed: int = 0) -> dict:
    streams_of = jax.random.split(jax.random.key(seed), 8)
    return {
        "latents": noise(streams_of[0], (TOKENS, Z), 1.0, 6.0, ((0, 128),)),
        "token_cell": draw_token_cell(jax.random.fold_in(streams_of[7], 71), 0),
        "frame_counts": ragged(streams_of[2], N_BAND, FRAMES, FCAP, 2).astype(jnp.int32),
        "in_kernel": noise(streams_of[3], (3, 3, 3, Z, C), (27 * Z) ** -0.5, 0.3125),
        "in_bias": noise(streams_of[4], (C,), 0.5, 3.0, (), jnp.float32),
        "mid_kernel": noise(streams_of[5], (3, 3, 3, C, C), (27 * C) ** -0.5, 0.0625),
        "mid_bias": noise(streams_of[6], (C,), 0.5, 3.0, (), jnp.float32),
    }


conv_layout = ("NDHWC", "DHWIO", "NDHWC")


def causal_conv(volume, kernel, bias):
    summed = lax.conv_general_dilated(volume[None], kernel, (1, 1, 1), [(2, 0), (1, 1), (1, 1)], dimension_numbers=conv_layout, preferred_element_type=jnp.float32)[0]
    return summed + bias


def reference(latents, token_cell, frame_counts, in_kernel, in_bias, mid_kernel, mid_bias):
    channels = latents.shape[1]
    grid = jnp.zeros((FRAMES * H * W, channels), latents.dtype).at[token_cell].set(latents)
    grid = grid.reshape(FRAMES, H, W, channels)
    first_conv = causal_conv(grid, in_kernel, in_bias)
    active = jax.nn.silu(first_conv).astype(jnp.bfloat16)
    mixed = causal_conv(active, mid_kernel, mid_bias).astype(jnp.bfloat16)
    counts = frame_counts.astype(jnp.int32)
    starts = (jnp.cumsum(counts) - counts).astype(jnp.int32)
    slots = jnp.arange(FCAP, dtype=jnp.int32)
    frame_index = (starts[:, None] + slots[None, :]).reshape(-1).astype(jnp.int32)
    live_slots = (slots[None, :] < counts[:, None]).reshape(-1)
    picked = jnp.take(mixed, jnp.clip(frame_index, 0, FRAMES - 1).astype(jnp.int32), axis=0)
    zeros_like = jnp.zeros_like(picked)
    return jnp.where(live_slots[:, None, None, None], picked, zeros_like)
```

```python
import functools

import jax
import jax.numpy as jnp
from jax import lax
from jax.experimental import pallas as pl
from jax.experimental.pallas import tpu as pltpu
from jax.sharding import PartitionSpec as P

W = 160
R = 4
FCAP = 4
Z = 16
C = 384
SPAN = 40
BANDS = 16
ROWS = 8
TOK = 840
LANES = 128
ACT_FRAMES = FCAP + 2
ACT_ROWS = R + 2
LAT_ROWS = R + 4
SLAB = R * W
K2 = 9 * C


def sort_kernel(counts, cell_ref, lat_ref, out_ref, flat):
    device = lax.axis_index("band") * ROWS + lax.axis_index("rows")
    cell = cell_ref[...]
    frame = ((cell >> 10) * 205) >> 10
    spot = cell - frame * (W * R * ROWS) - device * SPAN
    lat = lat_ref[...]
    zero = jnp.zeros_like(lat)
    frame_b = jnp.broadcast_to(frame, (Z, TOK))
    spread = jnp.concatenate(
        [jnp.where(frame_b == (f - FCAP), lat, zero) for f in range(32)], axis=0
    )
    spots = lax.broadcasted_iota(jnp.int32, (SPAN, TOK), 0)
    pick = jnp.where(spots == jnp.broadcast_to(spot, (SPAN, TOK)), 1.0, 0.0).astype(jnp.bfloat16)
    sorted_rows = lax.dot_general(
        pick, spread, (((1,), (1,)), ((), ())), preferred_element_type=jnp.float32
    )
    for tile in range(4):
        flat[tile] = sorted_rows[:, tile * LANES:(tile + 1) * LANES]
    lane = lax.broadcasted_iota(jnp.int32, (SPAN, LANES), 1)
    start = jnp.int32(0)
    for band in range(BANDS):
        tile = start // 8
        turn = (start - tile * 8) * Z
        back = jnp.where(turn == 0, 0, LANES - turn)
        left = pltpu.roll(flat[tile], back, 1)
        right = pltpu.roll(flat[jnp.minimum(tile + 1, 3)], back, 1)
        window = jnp.where(lane < LANES - turn, left, right)
        out_ref[band] = window.astype(jnp.bfloat16)
        start = start + counts[band]


def sort_tokens(counts, cells, latents):
    return pl.pallas_call(
        sort_kernel,
        in_specs=[
            pl.BlockSpec(memory_space=pltpu.SMEM),
            pl.BlockSpec(memory_space=pltpu.VMEM),
            pl.BlockSpec(memory_space=pltpu.VMEM),
        ],
        out_specs=pl.BlockSpec(memory_space=pltpu.VMEM),
        out_shape=jax.ShapeDtypeStruct((BANDS, SPAN, LANES), jnp.bfloat16),
        scratch_shapes=[pltpu.VMEM((4, SPAN, LANES), jnp.float32)],
        name="sort_tokens",
    )(counts, cells, latents)


def conv_kernel(
    counts, got_ref, w1_ref, b1_ref, b2_ref, w2_hbm, out_hbm,
    w2, flat, e01, e2, act, patches, outs, w2_sem, out_sem,
):
    band = lax.axis_index("band")
    rows = lax.axis_index("rows")
    fetch = pltpu.make_async_copy(w2_hbm, w2, w2_sem)
    fetch.start()
    start = jnp.int32(0)
    own = jnp.int32(0)
    for b in range(BANDS):
        start = start + jnp.where(b < band, counts[b], 0)
        own = own + jnp.where(b == band, counts[b], 0)

    lane = lax.broadcasted_iota(jnp.int32, (W, LANES), 1)
    low = lane < 64
    flat[:, 0:8, :] = jnp.zeros((2, 8, LANES), jnp.float32)
    flat[:, 168:176, :] = jnp.zeros((2, 8, LANES), jnp.float32)
    after = jnp.zeros((W, LANES), jnp.float32)
    for i in reversed(range(LAT_ROWS)):
        buf = i % 2
        for q in range(4):
            piece = got_ref[4 * (i % 2) + q, i // 2]
            flat[buf, 8 + SPAN * q:8 + SPAN * (q + 1), :] = piece.astype(jnp.float32)
        left = flat[buf, 7:167, :]
        mid = flat[buf, 8:168, :]
        right = flat[buf, 9:169, :]
        for pp in range(3):
            down = (LANES - 32 * pp) % LANES
            up = (64 + LANES - 32 * pp) % LANES
            first = jnp.where(low, pltpu.roll(left, down, 1), pltpu.roll(mid, up, 1))
            second = jnp.where(low, pltpu.roll(right, down, 1), pltpu.roll(after, up, 1))
            e01[pp, W * i:W * (i + 1), :] = first.astype(jnp.bfloat16)
            e2[pp, W * i:W * (i + 1), :] = second.astype(jnp.bfloat16)
        after = right

    act[:, 0:8, :] = jnp.zeros((3, 8, 2 * C), jnp.float32)
    act[:, 168:176, :] = jnp.zeros((3, 8, 2 * C), jnp.float32)

    def first_rows(i, carry):
        row = R * rows - 1 + i
        row_in = (row >= 0) & (row < R * ROWS)
        for pp in range(3):
            at = [pl.ds(pl.multiple_of(W * (i + k), W), W) for k in range(3)]
            lhs = jnp.concatenate(
                [e01[pp, at[0], :], e01[pp, at[1], :], e01[pp, at[2], :],
                 e2[pp, at[0], :], e2[pp, at[2], :]], axis=1)
            total = jnp.dot(lhs, w1_ref[...], preferred_element_type=jnp.float32)
            for half in range(2):
                p = 2 * pp + half
                cols = slice(half * C, (half + 1) * C)
                v = total[:, cols] + b1_ref[...]
                v = v / (1.0 + jnp.exp(-v))
                keep = row_in & (start - 2 + p >= 0)
                act[pp, 8:168, cols] = jnp.where(keep, v, 0.0)
                for e in range(3):
                    patches[p, at[0], e * C:(e + 1) * C] = (
                        act[pp, 7 + e:167 + e, cols].astype(jnp.bfloat16))
        return carry

    lax.fori_loop(0, ACT_ROWS, first_rows, 0)
    fetch.wait()

    def lhs_of(p):
        return jnp.concatenate(
            [patches[p, W * b:W * b + SLAB, :] for b in range(3)], axis=1)

    def pair(n0, carry):
        @pl.when(own > n0)
        def _():
            a0 = jnp.dot(lhs_of(n0), w2[0], preferred_element_type=jnp.float32)
            t = jnp.dot(
                lhs_of(n0 + 1), jnp.concatenate([w2[1], w2[0]], axis=1),
                preferred_element_type=jnp.float32)
            a0 += t[:, :C]
            a1 = t[:, C:]
            t = jnp.dot(
                lhs_of(n0 + 2), jnp.concatenate([w2[2], w2[1]], axis=1),
                preferred_element_type=jnp.float32)
            a0 += t[:, :C]
            a1 += t[:, C:]
            a1 += jnp.dot(lhs_of(n0 + 3), w2[2], preferred_element_type=jnp.float32)
            outs[n0] = (a0 + b2_ref[...]).astype(jnp.bfloat16)
            outs[n0 + 1] = jnp.where(own > n0 + 1, a1 + b2_ref[...], 0.0).astype(jnp.bfloat16)

        @pl.when(own <= n0)
        def _():
            outs[pl.ds(n0, 2)] = jnp.zeros((2, SLAB, C), jnp.bfloat16)

        pltpu.make_async_copy(
            outs.at[pl.ds(n0, 2)], out_hbm.at[pl.ds(n0, 2)], out_sem.at[n0 // 2]).start()
        return carry

    lax.fori_loop(0, 2, lambda k, c: pair(2 * k, c), 0)
    for k in range(2):
        pltpu.make_async_copy(
            outs.at[pl.ds(2 * k, 2)], out_hbm.at[pl.ds(2 * k, 2)], out_sem.at[k]).wait()


def convs(counts, got, w1, b1, b2, w2):
    vmem = pl.BlockSpec(memory_space=pltpu.VMEM)
    return pl.pallas_call(
        conv_kernel,
        in_specs=[
            pl.BlockSpec(memory_space=pltpu.SMEM), vmem, vmem, vmem, vmem,
            pl.BlockSpec(memory_space=pl.ANY),
        ],
        out_specs=pl.BlockSpec(memory_space=pl.ANY),
        out_shape=jax.ShapeDtypeStruct((FCAP, SLAB, C), jnp.bfloat16),
        scratch_shapes=[
            pltpu.VMEM((3, K2, C), jnp.bfloat16),
            pltpu.VMEM((2, 176, LANES), jnp.float32),
            pltpu.VMEM((3, LAT_ROWS * W, LANES), jnp.bfloat16),
            pltpu.VMEM((3, LAT_ROWS * W, LANES), jnp.bfloat16),
            pltpu.VMEM((3, 176, 2 * C), jnp.float32),
            pltpu.VMEM((ACT_FRAMES, ACT_ROWS * W, 3 * C), jnp.bfloat16),
            pltpu.VMEM((FCAP, SLAB, C), jnp.bfloat16),
            pltpu.SemaphoreType.DMA,
            pltpu.SemaphoreType.DMA((2,)),
        ],
        compiler_params=pltpu.CompilerParams(vmem_limit_bytes=56 * 1024 * 1024),
        name="two_convs",
    )(counts, got, w1, b1, b2, w2)


def frame_pair_kernel(in_kernel):
    taps = jnp.transpose(in_kernel, (1, 2, 0, 3, 4)).reshape(3, 3, 3 * Z, C)
    even = jnp.pad(taps, ((0, 0), (0, 0), (0, Z), (0, 0)))
    odd = jnp.pad(taps, ((0, 0), (0, 0), (Z, 0), (0, 0)))
    both = jnp.concatenate([even, odd], axis=-1)
    return jnp.concatenate(
        [both[:, :2].reshape(384, 2 * C), both[:, 2].reshape(192, 2 * C),
         jnp.zeros((64, 2 * C), in_kernel.dtype)], axis=0)


def per_device(latents, token_cell, frame_counts, in_kernel, in_bias, mid_kernel, mid_bias):
    windows = sort_tokens(frame_counts, token_cell.reshape(1, TOK), latents.T)
    by_band = lax.all_to_all(windows, "band", split_axis=0, concat_axis=0, tiled=True)
    edged = jnp.pad(by_band, ((1, 1), (0, 0), (0, 0)))
    spread = jnp.stack([edged[k:k + 15:2] for k in range(4)], axis=1)
    got = lax.all_to_all(spread, "rows", split_axis=0, concat_axis=0, tiled=True)
    out = convs(
        frame_counts, got, frame_pair_kernel(in_kernel), in_bias.reshape(1, C),
        mid_bias.reshape(1, C), mid_kernel.reshape(3, K2, C))
    return out.reshape(FCAP, R, W, C)


def solution(mesh):
    placed = (P(("band", "rows"), None), P(("band", "rows")), P(), P(), P(), P(), P())
    return jax.shard_map(
        per_device,
        mesh=mesh,
        in_specs=placed,
        out_specs=P("band", "rows", None, None),
        check_vma=False,
    )
```

```python
import functools

import jax
import jax.numpy as jnp
from jax import lax
from jax.experimental import pallas as pl
from jax.experimental.pallas import tpu as pltpu
from jax.sharding import PartitionSpec as P

W = 160
R = 4
FCAP = 4
Z = 16
C = 384
SPAN = 40
BANDS = 16
ROWS = 8
TOK = 840
LANES = 128
PHASES = 5
STEPS = W // PHASES
WIDE = W + 2 * STEPS
ACT_FRAMES = FCAP + 2
ACT_ROWS = R + 2
LAT_ROWS = R + 4
SLAB = R * W
K2 = 9 * C


def sort_kernel(counts, cell_ref, lat_ref, out_ref, flat):
    device = lax.axis_index("band") * ROWS + lax.axis_index("rows")
    cell = jnp.broadcast_to(cell_ref[...].reshape(1, TOK), (Z, TOK))
    frame = ((cell >> 10) * 205) >> 10
    spot = (cell - frame * (W * R * ROWS) - device * SPAN)[0:1]
    lat = lat_ref[...]
    zero = jnp.zeros_like(lat)
    spread = jnp.concatenate(
        [jnp.where(frame == (f - FCAP), lat, zero) for f in range(32)], axis=0
    )
    place = lax.broadcasted_iota(jnp.int32, (SPAN, TOK), 0)
    wanted = (place & 7) * PHASES + (place >> 3)
    pick = jnp.where(wanted == jnp.broadcast_to(spot, (SPAN, TOK)), 1.0, 0.0).astype(jnp.bfloat16)
    sorted_rows = lax.dot_general(
        pick, spread, (((1,), (1,)), ((), ())), preferred_element_type=jnp.float32
    )
    for tile in range(4):
        flat[tile] = sorted_rows[:, tile * LANES:(tile + 1) * LANES]
    lane = lax.broadcasted_iota(jnp.int32, (SPAN, LANES), 1)
    start = jnp.int32(0)
    for band in range(BANDS):
        tile = start // 8
        turn = (start - tile * 8) * Z
        back = jnp.where(turn == 0, 0, LANES - turn)
        left = pltpu.roll(flat[tile], back, 1)
        right = pltpu.roll(flat[jnp.minimum(tile + 1, 3)], back, 1)
        window = jnp.where(lane < LANES - turn, left, right)
        out_ref[band] = window.astype(jnp.bfloat16)
        start = start + counts[band]


def sort_tokens(counts, cells, latents):
    return pl.pallas_call(
        sort_kernel,
        in_specs=[
            pl.BlockSpec(memory_space=pltpu.SMEM),
            pl.BlockSpec(memory_space=pltpu.VMEM),
            pl.BlockSpec(memory_space=pltpu.VMEM),
        ],
        out_specs=pl.BlockSpec(memory_space=pltpu.VMEM),
        out_shape=jax.ShapeDtypeStruct((BANDS, SPAN, LANES), jnp.bfloat16),
        scratch_shapes=[pltpu.VMEM((4, SPAN, LANES), jnp.float32)],
        name="sort_tokens",
    )(counts, cells, latents)


def with_edges(rows):
    width = rows.shape[1]
    u = lax.broadcasted_iota(jnp.int32, (STEPS, width), 0)
    before = jnp.where(u == 0, 0.0, pltpu.roll(rows[W - STEPS:], 1, 0))
    after = jnp.where(u == STEPS - 1, 0.0, pltpu.roll(rows[:STEPS], STEPS - 1, 0))
    return jnp.concatenate([before, rows, after], axis=0)


def conv_kernel(
    counts, got_ref, w1_ref, b1_ref, b2_ref, w2_hbm, out_hbm,
    w2, e01, e2, patches, natural, outs, w2_sem, out_sem,
):
    band = lax.axis_index("band")
    rows = lax.axis_index("rows")
    fetch = pltpu.make_async_copy(w2_hbm, w2, w2_sem)
    fetch.start()
    start = jnp.int32(0)
    own = jnp.int32(0)
    for b in range(BANDS):
        start = start + jnp.where(b < band, counts[b], 0)
        own = own + jnp.where(b == band, counts[b], 0)

    lane = lax.broadcasted_iota(jnp.int32, (W, LANES), 1)
    low = lane < 64
    above = [jnp.zeros((W, LANES), jnp.float32)] * 4
    for i in reversed(range(LAT_ROWS)):
        pieces = [got_ref[4 * (i % 2) + q, i // 2].astype(jnp.float32) for q in range(4)]
        line = with_edges(jnp.concatenate(
            [pieces[q][8 * v:8 * v + 8] for v in range(PHASES) for q in range(4)], axis=0))
        turned = [line] + [pltpu.roll(line, 32 * k, 1) for k in range(1, 4)]
        for pp in range(3):
            down = (4 - pp) % 4
            up = (2 + 4 - pp) % 4
            first = jnp.where(low, turned[down][0:W], turned[up][STEPS:STEPS + W])
            second = jnp.where(low, turned[down][2 * STEPS:], above[up])
            e01[pp, i] = first.astype(jnp.bfloat16)
            e2[pp, i] = second.astype(jnp.bfloat16)
        above = [t[2 * STEPS:] for t in turned]

    def first_conv(pp, carry):
        def slab(ref, k):
            return ref[pp, k:k + ACT_ROWS].reshape(ACT_ROWS * W, LANES)

        lhs = jnp.concatenate(
            [slab(e01, 0), slab(e01, 1), slab(e01, 2), slab(e2, 0), slab(e2, 2)], axis=1)
        total = jnp.dot(lhs, w1_ref[...], preferred_element_type=jnp.float32)
        for i in range(ACT_ROWS):
            row = R * rows - 1 + i
            row_in = (row >= 0) & (row < R * ROWS)
            for half in range(2):
                p = 2 * pp + half
                keep = row_in & (start - 2 + p >= 0)
                scale = jnp.where(keep, jnp.float32(0.5), jnp.float32(0.0))
                v = total[W * i:W * (i + 1), half * C:(half + 1) * C] + b1_ref[...]
                h = v * scale
                h = h + h * jnp.tanh(h)
                patches[p, i] = with_edges(h).astype(jnp.bfloat16)
        return carry

    lax.fori_loop(0, 3, first_conv, 0)
    fetch.wait()

    def lhs_of(p):
        return jnp.concatenate(
            [patches[p, b:b + R, STEPS * e:STEPS * e + W].reshape(SLAB, C)
             for b in range(3) for e in range(3)], axis=1)

    def finish(slot, value, live):
        for y in range(R):
            for t in range(3):
                cols = slice(t * LANES, (t + 1) * LANES)
                for v in range(PHASES):
                    at = y * W + v * STEPS
                    natural[t, pl.ds(y * W + v, STEPS, stride=PHASES), :] = value[at:at + STEPS, cols]
        for t in range(3):
            cols = slice(t * LANES, (t + 1) * LANES)
            done = natural[t] + b2_ref[:, cols]
            if live is not None:
                done = jnp.where(live, done, 0.0)
            outs[slot, :, cols] = done.astype(jnp.bfloat16)

    def pair(n0, carry):
        @pl.when(own > n0)
        def _():
            a0 = jnp.dot(lhs_of(n0), w2[0], preferred_element_type=jnp.float32)
            t = jnp.dot(
                lhs_of(n0 + 1), jnp.concatenate([w2[1], w2[0]], axis=1),
                preferred_element_type=jnp.float32)
            a0 += t[:, :C]
            a1 = t[:, C:]
            t = jnp.dot(
                lhs_of(n0 + 2), jnp.concatenate([w2[2], w2[1]], axis=1),
                preferred_element_type=jnp.float32)
            finish(n0, a0 + t[:, :C], None)
            a1 += t[:, C:]
            a1 += jnp.dot(lhs_of(n0 + 3), w2[2], preferred_element_type=jnp.float32)
            finish(n0 + 1, a1, own > n0 + 1)

        @pl.when(own <= n0)
        def _():
            outs[pl.ds(n0, 2)] = jnp.zeros((2, SLAB, C), jnp.bfloat16)

        pltpu.make_async_copy(
            outs.at[pl.ds(n0, 2)], out_hbm.at[pl.ds(n0, 2)], out_sem.at[n0 // 2]).start()
        return carry

    lax.fori_loop(0, 2, lambda k, c: pair(2 * k, c), 0)
    for k in range(2):
        pltpu.make_async_copy(
            outs.at[pl.ds(2 * k, 2)], out_hbm.at[pl.ds(2 * k, 2)], out_sem.at[k]).wait()


def convs(counts, got, w1, b1, b2, w2):
    vmem = pl.BlockSpec(memory_space=pltpu.VMEM)
    return pl.pallas_call(
        conv_kernel,
        in_specs=[
            pl.BlockSpec(memory_space=pltpu.SMEM), vmem, vmem, vmem, vmem,
            pl.BlockSpec(memory_space=pl.ANY),
        ],
        out_specs=pl.BlockSpec(memory_space=pl.ANY),
        out_shape=jax.ShapeDtypeStruct((FCAP, SLAB, C), jnp.bfloat16),
        scratch_shapes=[
            pltpu.VMEM((3, K2, C), jnp.bfloat16),
            pltpu.VMEM((3, LAT_ROWS, W, LANES), jnp.bfloat16),
            pltpu.VMEM((3, LAT_ROWS, W, LANES), jnp.bfloat16),
            pltpu.VMEM((ACT_FRAMES, ACT_ROWS, WIDE, C), jnp.bfloat16),
            pltpu.VMEM((3, SLAB, LANES), jnp.float32),
            pltpu.VMEM((FCAP, SLAB, C), jnp.bfloat16),
            pltpu.SemaphoreType.DMA,
            pltpu.SemaphoreType.DMA((2,)),
        ],
        compiler_params=pltpu.CompilerParams(vmem_limit_bytes=36 * 1024 * 1024),
        name="two_convs",
    )(counts, got, w1, b1, b2, w2)


def frame_pair_kernel(in_kernel):
    taps = jnp.transpose(in_kernel, (1, 2, 0, 3, 4)).reshape(3, 3, 3 * Z, C)
    even = jnp.pad(taps, ((0, 0), (0, 0), (0, Z), (0, 0)))
    odd = jnp.pad(taps, ((0, 0), (0, 0), (Z, 0), (0, 0)))
    both = jnp.concatenate([even, odd], axis=-1)
    return jnp.concatenate(
        [both[:, :2].reshape(384, 2 * C), both[:, 2].reshape(192, 2 * C),
         jnp.zeros((64, 2 * C), in_kernel.dtype)], axis=0)


def per_device(latents, token_cell, frame_counts, in_kernel, in_bias, mid_kernel, mid_bias):
    windows = sort_tokens(frame_counts, token_cell, latents.T)
    by_band = lax.all_to_all(windows, "band", split_axis=0, concat_axis=0, tiled=True)
    edged = jnp.pad(by_band, ((1, 1), (0, 0), (0, 0)))
    spread = jnp.stack([edged[k:k + 15:2] for k in range(4)], axis=1)
    got = lax.all_to_all(spread, "rows", split_axis=0, concat_axis=0, tiled=True)
    out = convs(
        frame_counts, got, frame_pair_kernel(in_kernel), in_bias.reshape(1, C),
        mid_bias.reshape(1, C), mid_kernel.reshape(3, K2, C))
    return out.reshape(FCAP, R, W, C)


def solution(mesh):
    placed = (P(("band", "rows"), None), P(("band", "rows")), P(), P(), P(), P(), P())
    return jax.shard_map(
        per_device,
        mesh=mesh,
        in_specs=placed,
        out_specs=P("band", "rows", None, None),
        check_vma=False,
    )
```

```python
import functools

import jax
import jax.numpy as jnp
from jax import lax
from jax.experimental import pallas as pl
from jax.experimental.pallas import tpu as pltpu
from jax.sharding import PartitionSpec as P

W = 160
R = 4
FCAP = 4
Z = 16
C = 384
SPAN = 40
BANDS = 16
ROWS = 8
TOK = 840
LANES = 128
PHASES = 5
STEPS = W // PHASES
WIDE = W + 2 * STEPS
ACT_FRAMES = FCAP + 2
ACT_ROWS = R + 2
LAT_ROWS = R + 4
SLAB = R * W
K2 = 9 * C


def sort_kernel(counts, cell_ref, lat_ref, out_ref, flat):
    device = lax.axis_index("band") * ROWS + lax.axis_index("rows")
    cell = jnp.broadcast_to(cell_ref[...].reshape(1, TOK), (Z, TOK))
    frame = ((cell >> 10) * 205) >> 10
    spot = (cell - frame * (W * R * ROWS) - device * SPAN)[0:1]
    lat = lat_ref[...]
    zero = jnp.zeros_like(lat)
    spread = jnp.concatenate(
        [jnp.where(frame == (f - FCAP), lat, zero) for f in range(32)], axis=0
    )
    place = lax.broadcasted_iota(jnp.int32, (SPAN, TOK), 0)
    wanted = (place & 7) * PHASES + (place >> 3)
    pick = jnp.where(wanted == jnp.broadcast_to(spot, (SPAN, TOK)), 1.0, 0.0).astype(jnp.bfloat16)
    sorted_rows = lax.dot_general(
        pick, spread, (((1,), (1,)), ((), ())), preferred_element_type=jnp.float32
    )
    for tile in range(4):
        flat[tile] = sorted_rows[:, tile * LANES:(tile + 1) * LANES]
    lane = lax.broadcasted_iota(jnp.int32, (SPAN, LANES), 1)
    start = jnp.int32(0)
    for band in range(BANDS):
        tile = start // 8
        turn = (start - tile * 8) * Z
        back = jnp.where(turn == 0, 0, LANES - turn)
        left = pltpu.roll(flat[tile], back, 1)
        right = pltpu.roll(flat[jnp.minimum(tile + 1, 3)], back, 1)
        window = jnp.where(lane < LANES - turn, left, right)
        out_ref[band] = window.astype(jnp.bfloat16)
        start = start + counts[band]


def sort_tokens(counts, cells, latents):
    return pl.pallas_call(
        sort_kernel,
        in_specs=[
            pl.BlockSpec(memory_space=pltpu.SMEM),
            pl.BlockSpec(memory_space=pltpu.VMEM),
            pl.BlockSpec(memory_space=pltpu.VMEM),
        ],
        out_specs=pl.BlockSpec(memory_space=pltpu.VMEM),
        out_shape=jax.ShapeDtypeStruct((BANDS, SPAN, LANES), jnp.bfloat16),
        scratch_shapes=[pltpu.VMEM((4, SPAN, LANES), jnp.float32)],
        name="sort_tokens",
    )(counts, cells, latents)


def with_edges(rows):
    width = rows.shape[1]
    u = lax.broadcasted_iota(jnp.int32, (STEPS, width), 0)
    before = jnp.where(u == 0, 0.0, pltpu.roll(rows[W - STEPS:], 1, 0))
    after = jnp.where(u == STEPS - 1, 0.0, pltpu.roll(rows[:STEPS], STEPS - 1, 0))
    return jnp.concatenate([before, rows, after], axis=0)


def conv_kernel(
    counts, got_ref, w1_ref, b1_ref, b2_ref, w2_hbm, out_hbm,
    w2, e01, e2, patches, natural, outs, w2_sem, out_sem,
):
    band = lax.axis_index("band")
    rows = lax.axis_index("rows")
    fetch = pltpu.make_async_copy(w2_hbm, w2, w2_sem)
    fetch.start()
    start = jnp.int32(0)
    own = jnp.int32(0)
    for b in range(BANDS):
        start = start + jnp.where(b < band, counts[b], 0)
        own = own + jnp.where(b == band, counts[b], 0)

    lane = lax.broadcasted_iota(jnp.int32, (W, LANES), 1)
    low = lane < 64
    above = [jnp.zeros((W, LANES), jnp.float32)] * 4
    for i in reversed(range(LAT_ROWS)):
        pieces = [got_ref[4 * (i % 2) + q, i // 2].astype(jnp.float32) for q in range(4)]
        line = with_edges(jnp.concatenate(
            [pieces[q][8 * v:8 * v + 8] for v in range(PHASES) for q in range(4)], axis=0))
        turned = [line] + [pltpu.roll(line, 32 * k, 1) for k in range(1, 4)]
        for pp in range(3):
            down = (4 - pp) % 4
            up = (2 + 4 - pp) % 4
            first = jnp.where(low, turned[down][0:W], turned[up][STEPS:STEPS + W])
            second = jnp.where(low, turned[down][2 * STEPS:], above[up])
            e01[pp, i] = first.astype(jnp.bfloat16)
            e2[pp, i] = second.astype(jnp.bfloat16)
        above = [t[2 * STEPS:] for t in turned]

    def first_conv(pp, carry):
        def slab(ref, k):
            return ref[pp, k:k + ACT_ROWS].reshape(ACT_ROWS * W, LANES)

        lhs = jnp.concatenate(
            [slab(e01, 0), slab(e01, 1), slab(e01, 2), slab(e2, 0), slab(e2, 2)], axis=1)
        total = jnp.dot(lhs, w1_ref[...], preferred_element_type=jnp.float32)
        for i in range(ACT_ROWS):
            row = R * rows - 1 + i
            row_in = (row >= 0) & (row < R * ROWS)
            for half in range(2):
                p = 2 * pp + half
                keep = row_in & (start - 2 + p >= 0)
                scale = jnp.where(keep, jnp.float32(0.5), jnp.float32(0.0))
                v = total[W * i:W * (i + 1), half * C:(half + 1) * C] + b1_ref[...]
                h = v * scale
                h = h + h * jnp.tanh(h)
                patches[p, i] = with_edges(h).astype(jnp.bfloat16)
        return carry

    lax.fori_loop(0, 3, first_conv, 0)
    fetch.wait()

    def lhs_of(p):
        return jnp.concatenate(
            [patches[p, b:b + R, STEPS * e:STEPS * e + W].reshape(SLAB, C)
             for b in range(3) for e in range(3)], axis=1)

    def finish(slot, value, live):
        for y in range(R):
            for t in range(3):
                cols = slice(t * LANES, (t + 1) * LANES)
                for v in range(PHASES):
                    at = y * W + v * STEPS
                    natural[t, pl.ds(y * W + v, STEPS, stride=PHASES), :] = value[at:at + STEPS, cols]
        for t in range(3):
            cols = slice(t * LANES, (t + 1) * LANES)
            done = natural[t] + b2_ref[:, cols]
            if live is not None:
                done = jnp.where(live, done, 0.0)
            outs[slot, :, cols] = done.astype(jnp.bfloat16)

    def pair(n0, carry):
        @pl.when(own > n0)
        def _():
            a0 = jnp.dot(lhs_of(n0), w2[0], preferred_element_type=jnp.float32)
            t = jnp.dot(
                lhs_of(n0 + 1), jnp.concatenate([w2[1], w2[0]], axis=1),
                preferred_element_type=jnp.float32)
            a0 += t[:, :C]
            a1 = t[:, C:]
            t = jnp.dot(
                lhs_of(n0 + 2), jnp.concatenate([w2[2], w2[1]], axis=1),
                preferred_element_type=jnp.float32)
            finish(n0, a0 + t[:, :C], None)
            a1 += t[:, C:]
            a1 += jnp.dot(lhs_of(n0 + 3), w2[2], preferred_element_type=jnp.float32)
            finish(n0 + 1, a1, own > n0 + 1)

        @pl.when(own <= n0)
        def _():
            outs[pl.ds(n0, 2)] = jnp.zeros((2, SLAB, C), jnp.bfloat16)

        pltpu.make_async_copy(
            outs.at[pl.ds(n0, 2)], out_hbm.at[pl.ds(n0, 2)], out_sem.at[n0 // 2]).start()
        return carry

    lax.fori_loop(0, 2, lambda k, c: pair(2 * k, c), 0)
    for k in range(2):
        pltpu.make_async_copy(
            outs.at[pl.ds(2 * k, 2)], out_hbm.at[pl.ds(2 * k, 2)], out_sem.at[k]).wait()


def convs(counts, got, w1, b1, b2, w2):
    vmem = pl.BlockSpec(memory_space=pltpu.VMEM)
    return pl.pallas_call(
        conv_kernel,
        in_specs=[
            pl.BlockSpec(memory_space=pltpu.SMEM), vmem, vmem, vmem, vmem,
            pl.BlockSpec(memory_space=pltpu.HBM),
        ],
        out_specs=pl.BlockSpec(memory_space=pl.ANY),
        out_shape=jax.ShapeDtypeStruct((FCAP, SLAB, C), jnp.bfloat16),
        scratch_shapes=[
            pltpu.VMEM((3, K2, C), jnp.bfloat16),
            pltpu.VMEM((3, LAT_ROWS, W, LANES), jnp.bfloat16),
            pltpu.VMEM((3, LAT_ROWS, W, LANES), jnp.bfloat16),
            pltpu.VMEM((ACT_FRAMES, ACT_ROWS, WIDE, C), jnp.bfloat16),
            pltpu.VMEM((3, SLAB, LANES), jnp.float32),
            pltpu.VMEM((FCAP, SLAB, C), jnp.bfloat16),
            pltpu.SemaphoreType.DMA,
            pltpu.SemaphoreType.DMA((2,)),
        ],
        compiler_params=pltpu.CompilerParams(vmem_limit_bytes=50 * 1024 * 1024),
        name="two_convs",
    )(counts, got, w1, b1, b2, w2)


def frame_pair_kernel(in_kernel):
    taps = jnp.transpose(in_kernel, (1, 2, 0, 3, 4)).reshape(3, 3, 3 * Z, C)
    even = jnp.pad(taps, ((0, 0), (0, 0), (0, Z), (0, 0)))
    odd = jnp.pad(taps, ((0, 0), (0, 0), (Z, 0), (0, 0)))
    both = jnp.concatenate([even, odd], axis=-1)
    return jnp.concatenate(
        [both[:, :2].reshape(384, 2 * C), both[:, 2].reshape(192, 2 * C),
         jnp.zeros((64, 2 * C), in_kernel.dtype)], axis=0)


def per_device(latents, token_cell, frame_counts, in_kernel, in_bias, mid_kernel, mid_bias):
    windows = sort_tokens(frame_counts, token_cell, latents.T)
    by_band = lax.all_to_all(windows, "band", split_axis=0, concat_axis=0, tiled=True)
    edged = jnp.pad(by_band, ((1, 1), (0, 0), (0, 0)))
    spread = jnp.stack([edged[k:k + 15:2] for k in range(4)], axis=1)
    got = lax.all_to_all(spread, "rows", split_axis=0, concat_axis=0, tiled=True)
    out = convs(
        frame_counts, got, frame_pair_kernel(in_kernel), in_bias.reshape(1, C),
        mid_bias.reshape(1, C), mid_kernel.reshape(3, K2, C))
    return out.reshape(FCAP, R, W, C)


def solution(mesh):
    placed = (P(("band", "rows"), None), P(("band", "rows")), P(), P(), P(), P(), P())
    return jax.shard_map(
        per_device,
        mesh=mesh,
        in_specs=placed,
        out_specs=P("band", "rows", None, None),
        check_vma=False,
    )
```

```python
import functools

import jax
import jax.numpy as jnp
from jax import lax
from jax.experimental import pallas as pl
from jax.experimental.pallas import tpu as pltpu
from jax.sharding import PartitionSpec as P

W = 160
R = 4
FCAP = 4
Z = 16
C = 384
SPAN = 40
BANDS = 16
ROWS = 8
TOK = 840
LANES = 128
PHASES = 5
STEPS = W // PHASES
WIDE = W + 2 * STEPS
ACT_FRAMES = FCAP + 2
ACT_ROWS = R + 2
LAT_ROWS = R + 4
SLAB = R * W
K2 = 9 * C


def sort_kernel(counts, cell_ref, lat_ref, out_ref, flat):
    device = lax.axis_index("band") * ROWS + lax.axis_index("rows")
    cell = jnp.broadcast_to(cell_ref[...].reshape(1, TOK), (Z, TOK))
    frame = ((cell >> 10) * 205) >> 10
    spot = (cell - frame * (W * R * ROWS) - device * SPAN)[0:1]
    lat = lat_ref[...]
    zero = jnp.zeros_like(lat)
    spread = jnp.concatenate(
        [jnp.where(frame == (f - FCAP), lat, zero) for f in range(32)], axis=0
    )
    place = lax.broadcasted_iota(jnp.int32, (SPAN, TOK), 0)
    wanted = (place & 7) * PHASES + (place >> 3)
    pick = jnp.where(wanted == jnp.broadcast_to(spot, (SPAN, TOK)), 1.0, 0.0).astype(jnp.bfloat16)
    sorted_rows = lax.dot_general(
        pick, spread, (((1,), (1,)), ((), ())), preferred_element_type=jnp.float32
    )
    for tile in range(4):
        flat[tile] = sorted_rows[:, tile * LANES:(tile + 1) * LANES]
    lane = lax.broadcasted_iota(jnp.int32, (SPAN, LANES), 1)
    start = jnp.int32(0)
    for band in range(BANDS):
        tile = start // 8
        turn = (start - tile * 8) * Z
        back = jnp.where(turn == 0, 0, LANES - turn)
        left = pltpu.roll(flat[tile], back, 1)
        right = pltpu.roll(flat[jnp.minimum(tile + 1, 3)], back, 1)
        window = jnp.where(lane < LANES - turn, left, right)
        out_ref[band] = window.astype(jnp.bfloat16)
        start = start + counts[band]


def sort_tokens(counts, cells, latents):
    return pl.pallas_call(
        sort_kernel,
        in_specs=[
            pl.BlockSpec(memory_space=pltpu.SMEM),
            pl.BlockSpec(memory_space=pltpu.VMEM),
            pl.BlockSpec(memory_space=pltpu.VMEM),
        ],
        out_specs=pl.BlockSpec(memory_space=pltpu.VMEM),
        out_shape=jax.ShapeDtypeStruct((BANDS, SPAN, LANES), jnp.bfloat16),
        scratch_shapes=[pltpu.VMEM((4, SPAN, LANES), jnp.float32)],
        name="sort_tokens",
    )(counts, cells, latents)


def with_edges(rows):
    width = rows.shape[1]
    u = lax.broadcasted_iota(jnp.int32, (STEPS, width), 0)
    before = jnp.where(u == 0, 0.0, pltpu.roll(rows[W - STEPS:], 1, 0))
    after = jnp.where(u == STEPS - 1, 0.0, pltpu.roll(rows[:STEPS], STEPS - 1, 0))
    return jnp.concatenate([before, rows, after], axis=0)


def conv_kernel(
    counts, got_ref, w1_ref, b1_ref, b2_ref, mid_hbm, mix_hbm, out_hbm,
    w2, e01, e2, patches, mixed, natural, outs, w2_sem, out_sem,
):
    band = lax.axis_index("band")
    rows = lax.axis_index("rows")
    fetches = [
        pltpu.make_async_copy(mid_hbm.at[0], w2.at[0], w2_sem.at[0]),
        pltpu.make_async_copy(mid_hbm.at[2], w2.at[3], w2_sem.at[1]),
        pltpu.make_async_copy(mix_hbm, w2.at[1:3], w2_sem.at[2]),
    ]
    for fetch in fetches:
        fetch.start()
    start = jnp.int32(0)
    own = jnp.int32(0)
    for b in range(BANDS):
        start = start + jnp.where(b < band, counts[b], 0)
        own = own + jnp.where(b == band, counts[b], 0)

    lane = lax.broadcasted_iota(jnp.int32, (W, LANES), 1)
    low = lane < 64
    above = [jnp.zeros((W, LANES), jnp.float32)] * 4
    for i in reversed(range(LAT_ROWS)):
        pieces = [got_ref[4 * (i % 2) + q, i // 2].astype(jnp.float32) for q in range(4)]
        line = with_edges(jnp.concatenate(
            [pieces[q][8 * v:8 * v + 8] for v in range(PHASES) for q in range(4)], axis=0))
        turned = [line] + [pltpu.roll(line, 32 * k, 1) for k in range(1, 4)]
        for pp in range(3):
            down = (4 - pp) % 4
            up = (2 + 4 - pp) % 4
            first = jnp.where(low, turned[down][0:W], turned[up][STEPS:STEPS + W])
            second = jnp.where(low, turned[down][2 * STEPS:], above[up])
            e01[pp, i] = first.astype(jnp.bfloat16)
            e2[pp, i] = second.astype(jnp.bfloat16)
        above = [t[2 * STEPS:] for t in turned]

    def slab(ref, pp, k):
        return ref[pp, k:k + ACT_ROWS].reshape(ACT_ROWS * W, LANES)

    for pp in range(3):
        lhs = jnp.concatenate(
            [slab(e01, pp, 0), slab(e01, pp, 1), slab(e01, pp, 2),
             slab(e2, pp, 0), slab(e2, pp, 2)], axis=1)
        total = jnp.dot(lhs, w1_ref[...], preferred_element_type=jnp.float32)
        for i in range(ACT_ROWS):
            row = R * rows - 1 + i
            row_in = (row >= 0) & (row < R * ROWS)
            for half in range(2):
                p = 2 * pp + half
                keep = row_in & (start - 2 + p >= 0)
                scale = jnp.where(keep, jnp.float32(0.5), jnp.float32(0.0))
                v = total[W * i:W * (i + 1), half * C:(half + 1) * C] + b1_ref[...]
                h = v * scale
                h = h + h * jnp.tanh(h)
                patches[p, i] = with_edges(h).astype(jnp.bfloat16)

    for fetch in fetches:
        fetch.wait()

    def product(k):
        lhs = jnp.concatenate(
            [mixed[k, b:b + R, STEPS * e:STEPS * e + W].reshape(SLAB, C)
             for b in range(3) for e in range(3)], axis=1)
        return jnp.dot(lhs, w2[k], preferred_element_type=jnp.float32)

    def finish(slot, value, live):
        for y in range(R):
            for t in range(3):
                cols = slice(t * LANES, (t + 1) * LANES)
                for v in range(PHASES):
                    at = y * W + v * STEPS
                    natural[t, pl.ds(y * W + v, STEPS, stride=PHASES), :] = value[at:at + STEPS, cols]
        for t in range(3):
            cols = slice(t * LANES, (t + 1) * LANES)
            done = natural[t] + b2_ref[:, cols]
            if live is not None:
                done = jnp.where(live, done, 0.0)
            outs[slot, :, cols] = done.astype(jnp.bfloat16)

    def pair(n0, carry):
        @pl.when(own > n0)
        def _():
            mixed[0] = patches[n0] - patches[n0 + 2]
            mixed[1] = patches[n0 + 1] + patches[n0 + 2]
            mixed[2] = patches[n0 + 2] - patches[n0 + 1]
            mixed[3] = patches[n0 + 1] - patches[n0 + 3]
            m1 = product(1)
            m2 = product(2)
            finish(n0, product(0) + (m1 + m2), None)
            finish(n0 + 1, (m1 - m2) - product(3), own > n0 + 1)

        @pl.when(own <= n0)
        def _():
            outs[pl.ds(n0, 2)] = jnp.zeros((2, SLAB, C), jnp.bfloat16)

        pltpu.make_async_copy(
            outs.at[pl.ds(n0, 2)], out_hbm.at[pl.ds(n0, 2)], out_sem.at[n0 // 2]).start()
        return carry

    lax.fori_loop(0, 2, lambda k, c: pair(2 * k, c), 0)
    for k in range(2):
        pltpu.make_async_copy(
            outs.at[pl.ds(2 * k, 2)], out_hbm.at[pl.ds(2 * k, 2)], out_sem.at[k]).wait()


def convs(counts, got, w1, b1, b2, mid, mix):
    vmem = pl.BlockSpec(memory_space=pltpu.VMEM)
    return pl.pallas_call(
        conv_kernel,
        in_specs=[
            pl.BlockSpec(memory_space=pltpu.SMEM), vmem, vmem, vmem, vmem,
            pl.BlockSpec(memory_space=pl.ANY), pl.BlockSpec(memory_space=pl.ANY),
        ],
        out_specs=pl.BlockSpec(memory_space=pl.ANY),
        out_shape=jax.ShapeDtypeStruct((FCAP, SLAB, C), jnp.bfloat16),
        scratch_shapes=[
            pltpu.VMEM((4, K2, C), jnp.bfloat16),
            pltpu.VMEM((3, LAT_ROWS, W, LANES), jnp.bfloat16),
            pltpu.VMEM((3, LAT_ROWS, W, LANES), jnp.bfloat16),
            pltpu.VMEM((ACT_FRAMES, ACT_ROWS, WIDE, C), jnp.bfloat16),
            pltpu.VMEM((4, ACT_ROWS, WIDE, C), jnp.bfloat16),
            pltpu.VMEM((3, SLAB, LANES), jnp.float32),
            pltpu.VMEM((FCAP, SLAB, C), jnp.bfloat16),
            pltpu.SemaphoreType.DMA((3,)),
            pltpu.SemaphoreType.DMA((2,)),
        ],
        compiler_params=pltpu.CompilerParams(vmem_limit_bytes=50 * 1024 * 1024),
        name="two_convs",
    )(counts, got, w1, b1, b2, mid, mix)


def frame_pair_kernel(in_kernel):
    taps = jnp.transpose(in_kernel, (1, 2, 0, 3, 4)).reshape(3, 3, 3 * Z, C)
    even = jnp.pad(taps, ((0, 0), (0, 0), (0, Z), (0, 0)))
    odd = jnp.pad(taps, ((0, 0), (0, 0), (Z, 0), (0, 0)))
    both = jnp.concatenate([even, odd], axis=-1)
    return jnp.concatenate(
        [both[:, :2].reshape(384, 2 * C), both[:, 2].reshape(192, 2 * C),
         jnp.zeros((64, 2 * C), in_kernel.dtype)], axis=0)


def mix_kernel(mid_ref, out_ref):
    ends = mid_ref[0].astype(jnp.float32) + mid_ref[2].astype(jnp.float32)
    middle = mid_ref[1].astype(jnp.float32)
    out_ref[0] = (0.5 * (ends + middle)).astype(jnp.bfloat16)
    out_ref[1] = (0.5 * (ends - middle)).astype(jnp.bfloat16)


def time_mixes(mid):
    block = K2 // 9
    return pl.pallas_call(
        mix_kernel,
        grid=(9,),
        in_specs=[pl.BlockSpec((3, block, C), lambda k: (0, k, 0))],
        out_specs=pl.BlockSpec((2, block, C), lambda k: (0, k, 0)),
        out_shape=jax.ShapeDtypeStruct((2, K2, C), jnp.bfloat16),
        cost_estimate=pl.CostEstimate(
            flops=6 * K2 * C, bytes_accessed=10 * K2 * C, transcendentals=0),
        name="time_mixes",
    )(mid)


def per_device(latents, token_cell, frame_counts, in_kernel, in_bias, mid_kernel, mid_bias):
    windows = sort_tokens(frame_counts, token_cell, latents.T)
    by_band = lax.all_to_all(windows, "band", split_axis=0, concat_axis=0, tiled=True)
    mid = mid_kernel.reshape(3, K2, C)
    by_band, mix = lax.optimization_barrier((by_band, time_mixes(mid)))
    edged = jnp.pad(by_band, ((1, 1), (0, 0), (0, 0)))
    spread = jnp.stack([edged[k:k + 15:2] for k in range(4)], axis=1)
    got = lax.all_to_all(spread, "rows", split_axis=0, concat_axis=0, tiled=True)
    out = convs(
        frame_counts, got, frame_pair_kernel(in_kernel), in_bias.reshape(1, C),
        mid_bias.reshape(1, C), mid, mix)
    return out.reshape(FCAP, R, W, C)


def solution(mesh):
    placed = (P(("band", "rows"), None), P(("band", "rows")), P(), P(), P(), P(), P())
    return jax.shard_map(
        per_device,
        mesh=mesh,
        in_specs=placed,
        out_specs=P("band", "rows", None, None),
        check_vma=False,
    )
```

```python
import functools

import jax
import jax.numpy as jnp
from jax import lax
from jax.experimental import pallas as pl
from jax.experimental.pallas import tpu as pltpu
from jax.sharding import PartitionSpec as P

W = 160
R = 4
FCAP = 4
Z = 16
C = 384
SPAN = 40
BANDS = 16
ROWS = 8
TOK = 840
LANES = 128
PHASES = 5
STEPS = W // PHASES
WIDE = W + 2 * STEPS
ACT_FRAMES = FCAP + 2
ACT_ROWS = R + 2
LAT_ROWS = R + 4
SLAB = R * W
K2 = 9 * C
MIX_STEPS = 9


def sort_kernel(counts, cell_ref, lat_ref, out_ref, flat):
    device = lax.axis_index("band") * ROWS + lax.axis_index("rows")
    cell = jnp.broadcast_to(cell_ref[...].reshape(1, TOK), (Z, TOK))
    frame = ((cell >> 10) * 205) >> 10
    spot = (cell - frame * (W * R * ROWS) - device * SPAN)[0:1]
    lat = lat_ref[...]
    zero = jnp.zeros_like(lat)
    spread = jnp.concatenate(
        [jnp.where(frame == (f - FCAP), lat, zero) for f in range(32)], axis=0
    )
    place = lax.broadcasted_iota(jnp.int32, (SPAN, TOK), 0)
    wanted = (place & 7) * PHASES + (place >> 3)
    pick = jnp.where(wanted == jnp.broadcast_to(spot, (SPAN, TOK)), 1.0, 0.0).astype(jnp.bfloat16)
    sorted_rows = lax.dot_general(
        pick, spread, (((1,), (1,)), ((), ())), preferred_element_type=jnp.float32
    )
    for tile in range(4):
        flat[tile] = sorted_rows[:, tile * LANES:(tile + 1) * LANES]
    lane = lax.broadcasted_iota(jnp.int32, (SPAN, LANES), 1)
    start = jnp.int32(0)
    for band in range(BANDS):
        tile = start // 8
        turn = (start - tile * 8) * Z
        back = jnp.where(turn == 0, 0, LANES - turn)
        left = pltpu.roll(flat[tile], back, 1)
        right = pltpu.roll(flat[jnp.minimum(tile + 1, 3)], back, 1)
        window = jnp.where(lane < LANES - turn, left, right)
        out_ref[band] = window.astype(jnp.bfloat16)
        start = start + counts[band]


def sort_tokens(counts, cells, latents):
    return pl.pallas_call(
        sort_kernel,
        in_specs=[
            pl.BlockSpec(memory_space=pltpu.SMEM),
            pl.BlockSpec(memory_space=pltpu.VMEM),
            pl.BlockSpec(memory_space=pltpu.VMEM),
        ],
        out_specs=pl.BlockSpec(memory_space=pltpu.VMEM),
        out_shape=jax.ShapeDtypeStruct((BANDS, SPAN, LANES), jnp.bfloat16),
        scratch_shapes=[pltpu.VMEM((4, SPAN, LANES), jnp.float32)],
        name="sort_tokens",
    )(counts, cells, latents)


def with_edges(rows):
    width = rows.shape[1]
    u = lax.broadcasted_iota(jnp.int32, (STEPS, width), 0)
    before = jnp.where(u == 0, 0.0, pltpu.roll(rows[W - STEPS:], 1, 0))
    after = jnp.where(u == STEPS - 1, 0.0, pltpu.roll(rows[:STEPS], STEPS - 1, 0))
    return jnp.concatenate([before, rows, after], axis=0)


def conv_kernel(
    counts, got_ref, w1_ref, b1_ref, b2_ref, mid_hbm, mix_hbm, out_hbm,
    w2, e01, e2, patches, mixed, natural, outs, w2_sem, out_sem,
):
    band = lax.axis_index("band")
    rows = lax.axis_index("rows")
    fetches = [
        pltpu.make_async_copy(mid_hbm.at[0], w2.at[0], w2_sem.at[0]),
        pltpu.make_async_copy(mix_hbm.at[0], w2.at[1], w2_sem.at[1]),
        pltpu.make_async_copy(mix_hbm.at[1], w2.at[2], w2_sem.at[2]),
        pltpu.make_async_copy(mid_hbm.at[2], w2.at[3], w2_sem.at[3]),
    ]
    for fetch in fetches:
        fetch.start()
    start = jnp.int32(0)
    own = jnp.int32(0)
    for b in range(BANDS):
        start = start + jnp.where(b < band, counts[b], 0)
        own = own + jnp.where(b == band, counts[b], 0)

    bias1 = b1_ref[...].reshape(1, C)
    bias2 = b2_ref[...].reshape(1, C)
    lane = lax.broadcasted_iota(jnp.int32, (W, LANES), 1)
    low = lane < 64
    above = [jnp.zeros((W, LANES), jnp.float32)] * 4
    for i in reversed(range(LAT_ROWS)):
        pieces = [got_ref[4 * (i % 2) + q, i // 2].astype(jnp.float32) for q in range(4)]
        line = with_edges(jnp.concatenate(
            [pieces[q][8 * v:8 * v + 8] for v in range(PHASES) for q in range(4)], axis=0))
        turned = [line] + [pltpu.roll(line, 32 * k, 1) for k in range(1, 4)]
        for pp in range(3):
            down = (4 - pp) % 4
            up = (2 + 4 - pp) % 4
            first = jnp.where(low, turned[down][0:W], turned[up][STEPS:STEPS + W])
            second = jnp.where(low, turned[down][2 * STEPS:], above[up])
            e01[pp, i] = first.astype(jnp.bfloat16)
            e2[pp, i] = second.astype(jnp.bfloat16)
        above = [t[2 * STEPS:] for t in turned]

    def slab(ref, pp, k):
        return ref[pp, k:k + ACT_ROWS].reshape(ACT_ROWS * W, LANES)

    for pp in range(3):
        lhs = jnp.concatenate(
            [slab(e01, pp, 0), slab(e01, pp, 1), slab(e01, pp, 2),
             slab(e2, pp, 0), slab(e2, pp, 2)], axis=1)
        total = jnp.dot(lhs, w1_ref[...], preferred_element_type=jnp.float32)
        for i in range(ACT_ROWS):
            row = R * rows - 1 + i
            row_in = (row >= 0) & (row < R * ROWS)
            for half in range(2):
                p = 2 * pp + half
                keep = row_in & (start - 2 + p >= 0)
                scale = jnp.where(keep, jnp.float32(0.5), jnp.float32(0.0))
                v = total[W * i:W * (i + 1), half * C:(half + 1) * C] + bias1
                h = v * scale
                h = h + h * jnp.tanh(h)
                patches[p, i] = with_edges(h).astype(jnp.bfloat16)

    def product(k, fresh):
        if fresh and k < 2:
            for fetch in fetches[k:1 + 3 * k]:
                fetch.wait()
        lhs = jnp.concatenate(
            [mixed[k, b:b + R, STEPS * e:STEPS * e + W].reshape(SLAB, C)
             for b in range(3) for e in range(3)], axis=1)
        return jnp.dot(lhs, w2[k], preferred_element_type=jnp.float32)

    def finish(slot, value, live):
        for y in range(R):
            for t in range(3):
                cols = slice(t * LANES, (t + 1) * LANES)
                for v in range(PHASES):
                    at = y * W + v * STEPS
                    natural[t, pl.ds(y * W + v, STEPS, stride=PHASES), :] = value[at:at + STEPS, cols]
        for t in range(3):
            cols = slice(t * LANES, (t + 1) * LANES)
            done = natural[t] + bias2[:, cols]
            if live is not None:
                done = jnp.where(live, done, 0.0)
            outs[slot, :, cols] = done.astype(jnp.bfloat16)

    def pair(n0, fresh):
        mixed[0] = patches[n0] - patches[n0 + 2]
        mixed[1] = patches[n0 + 1] + patches[n0 + 2]
        mixed[2] = patches[n0 + 2] - patches[n0 + 1]
        mixed[3] = patches[n0 + 1] - patches[n0 + 3]
        m0 = product(0, fresh)
        m1 = product(1, fresh)
        m2 = product(2, fresh)
        finish(n0, m0 + 0.5 * (m1 + m2), None)
        finish(n0 + 1, 0.5 * (m1 - m2) - product(3, fresh), own > n0 + 1)

    def send(k):
        return pltpu.make_async_copy(
            outs.at[pl.ds(2 * k, 2)], out_hbm.at[pl.ds(2 * k, 2)], out_sem.at[k])

    pair(0, True)
    send(0).start()

    @pl.when(own > 2)
    def _():
        pair(2, False)

    @pl.when(own <= 2)
    def _():
        outs[2:4] = jnp.zeros((2, SLAB, C), jnp.bfloat16)

    send(1).start()
    send(0).wait()
    send(1).wait()


def convs(counts, got, w1, b1, b2, mid, mix):
    vmem = pl.BlockSpec(memory_space=pltpu.VMEM)
    return pl.pallas_call(
        conv_kernel,
        in_specs=[
            pl.BlockSpec(memory_space=pltpu.SMEM), vmem, vmem, vmem, vmem,
            pl.BlockSpec(memory_space=pl.ANY), pl.BlockSpec(memory_space=pl.ANY),
        ],
        out_specs=pl.BlockSpec(memory_space=pl.ANY),
        out_shape=jax.ShapeDtypeStruct((FCAP, SLAB, C), jnp.bfloat16),
        scratch_shapes=[
            pltpu.VMEM((4, K2, C), jnp.bfloat16),
            pltpu.VMEM((3, LAT_ROWS, W, LANES), jnp.bfloat16),
            pltpu.VMEM((3, LAT_ROWS, W, LANES), jnp.bfloat16),
            pltpu.VMEM((ACT_FRAMES, ACT_ROWS, WIDE, C), jnp.bfloat16),
            pltpu.VMEM((4, ACT_ROWS, WIDE, C), jnp.bfloat16),
            pltpu.VMEM((3, SLAB, LANES), jnp.float32),
            pltpu.VMEM((FCAP, SLAB, C), jnp.bfloat16),
            pltpu.SemaphoreType.DMA((4,)),
            pltpu.SemaphoreType.DMA((2,)),
        ],
        compiler_params=pltpu.CompilerParams(vmem_limit_bytes=50 * 1024 * 1024),
        name="two_convs",
    )(counts, got, w1, b1, b2, mid, mix)


def frame_pair_kernel(in_kernel):
    taps = jnp.transpose(in_kernel, (1, 2, 0, 3, 4)).reshape(3, 3, 3 * Z, C)
    even = jnp.pad(taps, ((0, 0), (0, 0), (0, Z), (0, 0)))
    odd = jnp.pad(taps, ((0, 0), (0, 0), (Z, 0), (0, 0)))
    both = jnp.concatenate([even, odd], axis=-1)
    return jnp.concatenate(
        [both[:, :2].reshape(384, 2 * C), both[:, 2].reshape(192, 2 * C),
         jnp.zeros((64, 2 * C), in_kernel.dtype)], axis=0)


def mix_kernel(mid_hbm, out_hbm, mids, mixes, in_sems, out_sems):
    block = K2 // MIX_STEPS

    def rows_of(k):
        return pl.ds(pl.multiple_of(k * block, block), block)

    def pull(k):
        return pltpu.make_async_copy(mid_hbm.at[:, rows_of(k)], mids.at[:, rows_of(k)], in_sems.at[k])

    def push(k):
        return pltpu.make_async_copy(mixes.at[:, rows_of(k)], out_hbm.at[:, rows_of(k)], out_sems.at[k])

    for k in range(MIX_STEPS):
        pull(k).start()

    def step(k, carry):
        pull(k).wait()
        ends = mids[0, rows_of(k)].astype(jnp.float32) + mids[2, rows_of(k)].astype(jnp.float32)
        middle = mids[1, rows_of(k)].astype(jnp.float32)
        mixes[0, rows_of(k)] = (ends + middle).astype(jnp.bfloat16)
        mixes[1, rows_of(k)] = (ends - middle).astype(jnp.bfloat16)
        push(k).start()
        return carry

    lax.fori_loop(0, MIX_STEPS, step, 0)
    for k in range(MIX_STEPS):
        push(k).wait()


def time_mixes(mid):
    return pl.pallas_call(
        mix_kernel,
        in_specs=[pl.BlockSpec(memory_space=pl.ANY)],
        out_specs=pl.BlockSpec(memory_space=pl.ANY),
        out_shape=jax.ShapeDtypeStruct((2, K2, C), jnp.bfloat16),
        scratch_shapes=[
            pltpu.VMEM((3, K2, C), jnp.bfloat16),
            pltpu.VMEM((2, K2, C), jnp.bfloat16),
            pltpu.SemaphoreType.DMA((MIX_STEPS,)),
            pltpu.SemaphoreType.DMA((MIX_STEPS,)),
        ],
        compiler_params=pltpu.CompilerParams(vmem_limit_bytes=52 * 1024 * 1024),
        cost_estimate=pl.CostEstimate(
            flops=6 * K2 * C, bytes_accessed=10 * K2 * C, transcendentals=0),
        name="time_mixes",
    )(mid)


def per_device(latents, token_cell, frame_counts, in_kernel, in_bias, mid_kernel, mid_bias):
    windows = sort_tokens(frame_counts, token_cell, latents.T)
    by_band = lax.all_to_all(windows, "band", split_axis=0, concat_axis=0, tiled=True)
    by_band, w1 = lax.optimization_barrier((by_band, frame_pair_kernel(in_kernel)))
    edged = jnp.pad(by_band, ((1, 1), (0, 0), (0, 0)))
    spread = jnp.stack([edged[k:k + 15:2] for k in range(4)], axis=1)
    spread, mid = lax.optimization_barrier((spread, mid_kernel.reshape(3, K2, C)))
    got = lax.all_to_all(spread, "rows", split_axis=0, concat_axis=0, tiled=True)
    out = convs(frame_counts, got, w1, in_bias, mid_bias, mid, time_mixes(mid))
    return out.reshape(FCAP, R, W, C)


def solution(mesh):
    placed = (P(("band", "rows"), None), P(("band", "rows")), P(), P(), P(), P(), P())
    return jax.shard_map(
        per_device,
        mesh=mesh,
        in_specs=placed,
        out_specs=P("band", "rows", None, None),
        check_vma=False,
    )
```

```python
import functools

import jax
import jax.numpy as jnp
from jax import lax
from jax.experimental import pallas as pl
from jax.experimental.pallas import tpu as pltpu
from jax.sharding import PartitionSpec as P

W = 160
R = 4
FCAP = 4
Z = 16
C = 384
SPAN = 40
BANDS = 16
ROWS = 8
TOK = 840
LANES = 128
PHASES = 5
STEPS = W // PHASES
WIDE = W + 2 * STEPS
ACT_FRAMES = FCAP + 2
ACT_ROWS = R + 2
LAT_ROWS = R + 4
SLAB = R * W
K2 = 9 * C
MIX_STEPS = 9


def sort_kernel(counts, cell_ref, lat_ref, out_ref, flat):
    device = lax.axis_index("band") * ROWS + lax.axis_index("rows")
    cell = jnp.broadcast_to(cell_ref[...].reshape(1, TOK), (Z, TOK))
    frame = ((cell >> 10) * 205) >> 10
    spot = (cell - frame * (W * R * ROWS) - device * SPAN)[0:1]
    lat = lat_ref[...]
    zero = jnp.zeros_like(lat)
    spread = jnp.concatenate(
        [jnp.where(frame == (f - FCAP), lat, zero) for f in range(32)], axis=0
    )
    place = lax.broadcasted_iota(jnp.int32, (SPAN, TOK), 0)
    wanted = (place & 7) * PHASES + (place >> 3)
    pick = jnp.where(wanted == jnp.broadcast_to(spot, (SPAN, TOK)), 1.0, 0.0).astype(jnp.bfloat16)
    sorted_rows = lax.dot_general(
        pick, spread, (((1,), (1,)), ((), ())), preferred_element_type=jnp.float32
    )
    for tile in range(4):
        flat[tile] = sorted_rows[:, tile * LANES:(tile + 1) * LANES]
    lane = lax.broadcasted_iota(jnp.int32, (SPAN, LANES), 1)
    start = jnp.int32(0)
    for band in range(BANDS):
        tile = start // 8
        turn = (start - tile * 8) * Z
        back = jnp.where(turn == 0, 0, LANES - turn)
        left = pltpu.roll(flat[tile], back, 1)
        right = pltpu.roll(flat[jnp.minimum(tile + 1, 3)], back, 1)
        window = jnp.where(lane < LANES - turn, left, right)
        out_ref[band] = window.astype(jnp.bfloat16)
        start = start + counts[band]


def sort_tokens(counts, cells, latents):
    return pl.pallas_call(
        sort_kernel,
        in_specs=[
            pl.BlockSpec(memory_space=pltpu.SMEM),
            pl.BlockSpec(memory_space=pltpu.VMEM),
            pl.BlockSpec(memory_space=pltpu.VMEM),
        ],
        out_specs=pl.BlockSpec(memory_space=pltpu.VMEM),
        out_shape=jax.ShapeDtypeStruct((BANDS, SPAN, LANES), jnp.bfloat16),
        scratch_shapes=[pltpu.VMEM((4, SPAN, LANES), jnp.float32)],
        name="sort_tokens",
    )(counts, cells, latents)


def with_edges(rows):
    width = rows.shape[1]
    u = lax.broadcasted_iota(jnp.int32, (STEPS, width), 0)
    before = jnp.where(u == 0, 0.0, pltpu.roll(rows[W - STEPS:], 1, 0))
    after = jnp.where(u == STEPS - 1, 0.0, pltpu.roll(rows[:STEPS], STEPS - 1, 0))
    return jnp.concatenate([before, rows, after], axis=0)


def conv_kernel(
    counts, got_ref, w1_ref, b1_ref, b2_ref, mid_hbm, mix_hbm, out_hbm,
    w2, e01, e2, patches, mixed, natural, outs, w2_sem, out_sem,
):
    band = lax.axis_index("band")
    rows = lax.axis_index("rows")
    fetches = [
        pltpu.make_async_copy(mid_hbm.at[0], w2.at[0], w2_sem.at[0]),
        pltpu.make_async_copy(mix_hbm.at[0], w2.at[1], w2_sem.at[1]),
        pltpu.make_async_copy(mix_hbm.at[1], w2.at[2], w2_sem.at[2]),
        pltpu.make_async_copy(mid_hbm.at[2], w2.at[3], w2_sem.at[3]),
    ]
    for fetch in fetches:
        fetch.start()
    start = jnp.int32(0)
    own = jnp.int32(0)
    for b in range(BANDS):
        start = start + jnp.where(b < band, counts[b], 0)
        own = own + jnp.where(b == band, counts[b], 0)

    bias1 = b1_ref[...].reshape(1, C)
    bias2 = b2_ref[...].reshape(1, C)
    lane = lax.broadcasted_iota(jnp.int32, (W, LANES), 1)
    low = lane < 64
    above = [jnp.zeros((W, LANES), jnp.float32)] * 4
    for i in reversed(range(LAT_ROWS)):
        pieces = [got_ref[4 * (i % 2) + q, i // 2].astype(jnp.float32) for q in range(4)]
        line = with_edges(jnp.concatenate(
            [pieces[q][8 * v:8 * v + 8] for v in range(PHASES) for q in range(4)], axis=0))
        turned = [line] + [pltpu.roll(line, 32 * k, 1) for k in range(1, 4)]
        for pp in range(3):
            down = (4 - pp) % 4
            up = (2 + 4 - pp) % 4
            first = jnp.where(low, turned[down][0:W], turned[up][STEPS:STEPS + W])
            second = jnp.where(low, turned[down][2 * STEPS:], above[up])
            e01[pp, i] = first.astype(jnp.bfloat16)
            e2[pp, i] = second.astype(jnp.bfloat16)
        above = [t[2 * STEPS:] for t in turned]

    def slab(ref, pp, k):
        return ref[pp, k:k + ACT_ROWS].reshape(ACT_ROWS * W, LANES)

    def first_conv(pp, carry):
        lhs = jnp.concatenate(
            [slab(e01, pp, 0), slab(e01, pp, 1), slab(e01, pp, 2),
             slab(e2, pp, 0), slab(e2, pp, 2)], axis=1)
        total = jnp.dot(lhs, w1_ref[...], preferred_element_type=jnp.float32)
        for i in range(ACT_ROWS):
            row = R * rows - 1 + i
            row_in = (row >= 0) & (row < R * ROWS)
            for half in range(2):
                p = 2 * pp + half
                keep = row_in & (start - 2 + p >= 0)
                scale = jnp.where(keep, jnp.float32(0.5), jnp.float32(0.0))
                v = total[W * i:W * (i + 1), half * C:(half + 1) * C] + bias1
                h = v * scale
                h = h + h * jnp.tanh(h)
                patches[p, i] = with_edges(h).astype(jnp.bfloat16)
        return carry

    lax.fori_loop(0, 3, first_conv, 0)

    for fetch in fetches:
        fetch.wait()

    def product(k):
        lhs = jnp.concatenate(
            [mixed[k, b:b + R, STEPS * e:STEPS * e + W].reshape(SLAB, C)
             for b in range(3) for e in range(3)], axis=1)
        return jnp.dot(lhs, w2[k], preferred_element_type=jnp.float32)

    def finish(slot, value, live):
        for y in range(R):
            for t in range(3):
                cols = slice(t * LANES, (t + 1) * LANES)
                for v in range(PHASES):
                    at = y * W + v * STEPS
                    natural[t, pl.ds(y * W + v, STEPS, stride=PHASES), :] = value[at:at + STEPS, cols]
        for t in range(3):
            cols = slice(t * LANES, (t + 1) * LANES)
            done = natural[t] + bias2[:, cols]
            if live is not None:
                done = jnp.where(live, done, 0.0)
            outs[slot, :, cols] = done.astype(jnp.bfloat16)

    def pair(n0):
        mixed[0] = patches[n0] - patches[n0 + 2]
        mixed[1] = patches[n0 + 1] + patches[n0 + 2]
        mixed[2] = patches[n0 + 2] - patches[n0 + 1]
        mixed[3] = patches[n0 + 1] - patches[n0 + 3]
        m0 = product(0)
        m1 = product(1)
        m2 = product(2)
        finish(n0, m0 + 0.5 * (m1 + m2), None)
        finish(n0 + 1, 0.5 * (m1 - m2) - product(3), own > n0 + 1)

    def send(k):
        return pltpu.make_async_copy(
            outs.at[pl.ds(2 * k, 2)], out_hbm.at[pl.ds(2 * k, 2)], out_sem.at[k])

    def slots(k, carry):
        @pl.when(own > 2 * k)
        def _():
            pair(2 * k)

        @pl.when(own <= 2 * k)
        def _():
            outs[pl.ds(2 * k, 2)] = jnp.zeros((2, SLAB, C), jnp.bfloat16)

        send(k).start()
        return carry

    lax.fori_loop(0, 2, slots, 0)
    send(0).wait()
    send(1).wait()


def convs(counts, got, w1, b1, b2, mid, mix):
    vmem = pl.BlockSpec(memory_space=pltpu.VMEM)
    return pl.pallas_call(
        conv_kernel,
        in_specs=[
            pl.BlockSpec(memory_space=pltpu.SMEM), vmem, vmem, vmem, vmem,
            pl.BlockSpec(memory_space=pl.ANY), pl.BlockSpec(memory_space=pl.ANY),
        ],
        out_specs=pl.BlockSpec(memory_space=pl.ANY),
        out_shape=jax.ShapeDtypeStruct((FCAP, SLAB, C), jnp.bfloat16),
        scratch_shapes=[
            pltpu.VMEM((4, K2, C), jnp.bfloat16),
            pltpu.VMEM((3, LAT_ROWS, W, LANES), jnp.bfloat16),
            pltpu.VMEM((3, LAT_ROWS, W, LANES), jnp.bfloat16),
            pltpu.VMEM((ACT_FRAMES, ACT_ROWS, WIDE, C), jnp.bfloat16),
            pltpu.VMEM((4, ACT_ROWS, WIDE, C), jnp.bfloat16),
            pltpu.VMEM((3, SLAB, LANES), jnp.float32),
            pltpu.VMEM((FCAP, SLAB, C), jnp.bfloat16),
            pltpu.SemaphoreType.DMA((4,)),
            pltpu.SemaphoreType.DMA((2,)),
        ],
        compiler_params=pltpu.CompilerParams(vmem_limit_bytes=50 * 1024 * 1024),
        name="two_convs",
    )(counts, got, w1, b1, b2, mid, mix)


def frame_pair_kernel(in_kernel):
    taps = jnp.transpose(in_kernel, (1, 2, 0, 3, 4)).reshape(3, 3, 3 * Z, C)
    even = jnp.pad(taps, ((0, 0), (0, 0), (0, Z), (0, 0)))
    odd = jnp.pad(taps, ((0, 0), (0, 0), (Z, 0), (0, 0)))
    both = jnp.concatenate([even, odd], axis=-1)
    return jnp.concatenate(
        [both[:, :2].reshape(384, 2 * C), both[:, 2].reshape(192, 2 * C),
         jnp.zeros((64, 2 * C), in_kernel.dtype)], axis=0)


def mix_kernel(mid_hbm, out_hbm, mids, mixes, in_sems, out_sems):
    block = K2 // MIX_STEPS

    def rows_of(k):
        return pl.ds(pl.multiple_of(k * block, block), block)

    def pull(k):
        return pltpu.make_async_copy(mid_hbm.at[:, rows_of(k)], mids.at[:, rows_of(k)], in_sems.at[k])

    def push(k):
        return pltpu.make_async_copy(mixes.at[:, rows_of(k)], out_hbm.at[:, rows_of(k)], out_sems.at[k])

    for k in range(MIX_STEPS):
        pull(k).start()

    def step(k, carry):
        pull(k).wait()
        ends = mids[0, rows_of(k)].astype(jnp.float32) + mids[2, rows_of(k)].astype(jnp.float32)
        middle = mids[1, rows_of(k)].astype(jnp.float32)
        mixes[0, rows_of(k)] = (ends + middle).astype(jnp.bfloat16)
        mixes[1, rows_of(k)] = (ends - middle).astype(jnp.bfloat16)
        push(k).start()
        return carry

    lax.fori_loop(0, MIX_STEPS, step, 0)
    for k in range(MIX_STEPS):
        push(k).wait()


def time_mixes(mid):
    return pl.pallas_call(
        mix_kernel,
        in_specs=[pl.BlockSpec(memory_space=pl.ANY)],
        out_specs=pl.BlockSpec(memory_space=pl.ANY),
        out_shape=jax.ShapeDtypeStruct((2, K2, C), jnp.bfloat16),
        scratch_shapes=[
            pltpu.VMEM((3, K2, C), jnp.bfloat16),
            pltpu.VMEM((2, K2, C), jnp.bfloat16),
            pltpu.SemaphoreType.DMA((MIX_STEPS,)),
            pltpu.SemaphoreType.DMA((MIX_STEPS,)),
        ],
        compiler_params=pltpu.CompilerParams(vmem_limit_bytes=52 * 1024 * 1024),
        cost_estimate=pl.CostEstimate(
            flops=6 * K2 * C, bytes_accessed=10 * K2 * C, transcendentals=0),
        name="time_mixes",
    )(mid)


def per_device(latents, token_cell, frame_counts, in_kernel, in_bias, mid_kernel, mid_bias):
    windows = sort_tokens(frame_counts, token_cell, latents.T)
    by_band = lax.all_to_all(windows, "band", split_axis=0, concat_axis=0, tiled=True)
    by_band, w1 = lax.optimization_barrier((by_band, frame_pair_kernel(in_kernel)))
    edged = jnp.pad(by_band, ((1, 1), (0, 0), (0, 0)))
    spread = jnp.stack([edged[k:k + 15:2] for k in range(4)], axis=1)
    spread, mid = lax.optimization_barrier((spread, mid_kernel.reshape(3, K2, C)))
    got = lax.all_to_all(spread, "rows", split_axis=0, concat_axis=0, tiled=True)
    out = convs(frame_counts, got, w1, in_bias, mid_bias, mid, time_mixes(mid))
    return out.reshape(FCAP, R, W, C)


def solution(mesh):
    placed = (P(("band", "rows"), None), P(("band", "rows")), P(), P(), P(), P(), P())
    return jax.shard_map(
        per_device,
        mesh=mesh,
        in_specs=placed,
        out_specs=P("band", "rows", None, None),
        check_vma=False,
    )
```

```python
import functools

import jax
import jax.numpy as jnp
from jax import lax
from jax.experimental import pallas as pl
from jax.experimental.pallas import tpu as pltpu
from jax.sharding import PartitionSpec as P

W = 160
R = 4
FCAP = 4
Z = 16
C = 384
SPAN = 40
BANDS = 16
ROWS = 8
TOK = 840
LANES = 128
PHASES = 5
STEPS = W // PHASES
WIDE = W + 2 * STEPS
ACT_FRAMES = FCAP + 2
ACT_ROWS = R + 2
LAT_ROWS = R + 4
SLAB = R * W
K2 = 9 * C
MIX_STEPS = 9


def sort_kernel(counts, cell_ref, lat_ref, out_ref, flat):
    device = lax.axis_index("band") * ROWS + lax.axis_index("rows")
    cell = jnp.broadcast_to(cell_ref[...].reshape(1, TOK), (Z, TOK))
    frame = ((cell >> 10) * 205) >> 10
    spot = (cell - frame * (W * R * ROWS) - device * SPAN)[0:1]
    lat = lat_ref[...]
    zero = jnp.zeros_like(lat)
    spread = jnp.concatenate(
        [jnp.where(frame == (f - FCAP), lat, zero) for f in range(32)], axis=0
    )
    place = lax.broadcasted_iota(jnp.int32, (SPAN, TOK), 0)
    wanted = (place & 7) * PHASES + (place >> 3)
    pick = jnp.where(wanted == jnp.broadcast_to(spot, (SPAN, TOK)), 1.0, 0.0).astype(jnp.bfloat16)
    sorted_rows = lax.dot_general(
        pick, spread, (((1,), (1,)), ((), ())), preferred_element_type=jnp.float32
    )
    for tile in range(4):
        flat[tile] = sorted_rows[:, tile * LANES:(tile + 1) * LANES]
    lane = lax.broadcasted_iota(jnp.int32, (SPAN, LANES), 1)
    start = jnp.int32(0)
    for band in range(BANDS):
        tile = start // 8
        turn = (start - tile * 8) * Z
        back = jnp.where(turn == 0, 0, LANES - turn)
        left = pltpu.roll(flat[tile], back, 1)
        right = pltpu.roll(flat[jnp.minimum(tile + 1, 3)], back, 1)
        window = jnp.where(lane < LANES - turn, left, right)
        out_ref[band] = window.astype(jnp.bfloat16)
        start = start + counts[band]


def sort_tokens(counts, cells, latents):
    return pl.pallas_call(
        sort_kernel,
        in_specs=[
            pl.BlockSpec(memory_space=pltpu.SMEM),
            pl.BlockSpec(memory_space=pltpu.VMEM),
            pl.BlockSpec(memory_space=pltpu.VMEM),
        ],
        out_specs=pl.BlockSpec(memory_space=pltpu.VMEM),
        out_shape=jax.ShapeDtypeStruct((BANDS, SPAN, LANES), jnp.bfloat16),
        scratch_shapes=[pltpu.VMEM((4, SPAN, LANES), jnp.float32)],
        name="sort_tokens",
    )(counts, cells, latents)


def with_edges(rows):
    width = rows.shape[1]
    u = lax.broadcasted_iota(jnp.int32, (STEPS, width), 0)
    before = jnp.where(u == 0, 0.0, pltpu.roll(rows[W - STEPS:], 1, 0))
    after = jnp.where(u == STEPS - 1, 0.0, pltpu.roll(rows[:STEPS], STEPS - 1, 0))
    return jnp.concatenate([before, rows, after], axis=0)


def conv_kernel(
    counts, got_ref, w1_ref, b1_ref, b2_ref, mid_hbm, mix_hbm, out_hbm,
    w2, e01, e2, patches, mixed, natural, outs, w2_sem, out_sem,
):
    band = lax.axis_index("band")
    rows = lax.axis_index("rows")
    fetches = [
        pltpu.make_async_copy(mid_hbm.at[0], w2.at[0], w2_sem.at[0]),
        pltpu.make_async_copy(mix_hbm.at[0], w2.at[1], w2_sem.at[1]),
        pltpu.make_async_copy(mix_hbm.at[1], w2.at[2], w2_sem.at[2]),
        pltpu.make_async_copy(mid_hbm.at[2], w2.at[3], w2_sem.at[3]),
    ]
    for fetch in fetches:
        fetch.start()
    start = jnp.int32(0)
    own = jnp.int32(0)
    for b in range(BANDS):
        start = start + jnp.where(b < band, counts[b], 0)
        own = own + jnp.where(b == band, counts[b], 0)

    bias1 = b1_ref[...].reshape(1, C)
    bias2 = b2_ref[...].reshape(1, C)
    lane = lax.broadcasted_iota(jnp.int32, (W, LANES), 1)
    low = lane < 64
    above = [jnp.zeros((W, LANES), jnp.float32)] * 4
    for i in reversed(range(LAT_ROWS)):
        pieces = [got_ref[4 * (i % 2) + q, i // 2].astype(jnp.float32) for q in range(4)]
        line = with_edges(jnp.concatenate(
            [pieces[q][8 * v:8 * v + 8] for v in range(PHASES) for q in range(4)], axis=0))
        turned = [line] + [pltpu.roll(line, 32 * k, 1) for k in range(1, 4)]
        for pp in range(3):
            down = (4 - pp) % 4
            up = (2 + 4 - pp) % 4
            first = jnp.where(low, turned[down][0:W], turned[up][STEPS:STEPS + W])
            second = jnp.where(low, turned[down][2 * STEPS:], above[up])
            e01[pp, i] = first.astype(jnp.bfloat16)
            e2[pp, i] = second.astype(jnp.bfloat16)
        above = [t[2 * STEPS:] for t in turned]

    def slab(ref, pp, k):
        return ref[pp, k:k + ACT_ROWS].reshape(ACT_ROWS * W, LANES)

    def first_conv(pp, carry):
        lhs = jnp.concatenate(
            [slab(e01, pp, 0), slab(e01, pp, 1), slab(e01, pp, 2),
             slab(e2, pp, 0), slab(e2, pp, 2)], axis=1)
        total = jnp.dot(lhs, w1_ref[...], preferred_element_type=jnp.float32)
        for i in range(ACT_ROWS):
            row = R * rows - 1 + i
            row_in = (row >= 0) & (row < R * ROWS)
            for half in range(2):
                p = 2 * pp + half
                keep = row_in & (start - 2 + p >= 0)
                scale = jnp.where(keep, jnp.float32(0.5), jnp.float32(0.0))
                v = total[W * i:W * (i + 1), half * C:(half + 1) * C] + bias1
                h = v * scale
                h = h + h * jnp.tanh(h)
                patches[p, i] = with_edges(h).astype(jnp.bfloat16)
        return carry

    lax.fori_loop(0, 3, first_conv, 0)

    for fetch in fetches:
        fetch.wait()

    def product(k):
        lhs = jnp.concatenate(
            [mixed[k, b:b + R, STEPS * e:STEPS * e + W].reshape(SLAB, C)
             for b in range(3) for e in range(3)], axis=1)
        return jnp.dot(lhs, w2[k], preferred_element_type=jnp.float32)

    def finish(slot, value, live):
        for y in range(R):
            for t in range(3):
                cols = slice(t * LANES, (t + 1) * LANES)
                for v in range(PHASES):
                    at = y * W + v * STEPS
                    natural[t, pl.ds(y * W + v, STEPS, stride=PHASES), :] = value[at:at + STEPS, cols]
        for t in range(3):
            cols = slice(t * LANES, (t + 1) * LANES)
            done = natural[t, 0:SLAB] + bias2[:, cols]
            if live is not None:
                done = jnp.where(live, done, 0.0)
            outs[slot, :, cols] = done.astype(jnp.bfloat16)

    def send(slot):
        return pltpu.make_async_copy(outs.at[slot], out_hbm.at[slot], out_sem.at[slot])

    def pair(n0):
        mixed[0] = patches[n0] - patches[n0 + 2]
        mixed[1] = patches[n0 + 1] + patches[n0 + 2]
        mixed[2] = patches[n0 + 2] - patches[n0 + 1]
        mixed[3] = patches[n0 + 1] - patches[n0 + 3]
        m0 = product(0)
        m1 = product(1)
        m2 = product(2)
        finish(n0, m0 + 0.5 * (m1 + m2), None)
        send(n0).start()
        finish(n0 + 1, 0.5 * (m1 - m2) - product(3), own > n0 + 1)
        send(n0 + 1).start()

    def slots(k, carry):
        @pl.when(own > 2 * k)
        def _():
            pair(2 * k)

        @pl.when(own <= 2 * k)
        def _():
            outs[pl.ds(2 * k, 2)] = jnp.zeros((2, SLAB, C), jnp.bfloat16)
            send(2 * k).start()
            send(2 * k + 1).start()

        return carry

    lax.fori_loop(0, 2, slots, 0)
    for slot in range(FCAP):
        send(slot).wait()


def convs(counts, got, w1, b1, b2, mid, mix):
    vmem = pl.BlockSpec(memory_space=pltpu.VMEM)
    return pl.pallas_call(
        conv_kernel,
        in_specs=[
            pl.BlockSpec(memory_space=pltpu.SMEM), vmem, vmem, vmem, vmem,
            pl.BlockSpec(memory_space=pl.ANY), pl.BlockSpec(memory_space=pl.ANY),
        ],
        out_specs=pl.BlockSpec(memory_space=pl.ANY),
        out_shape=jax.ShapeDtypeStruct((FCAP, SLAB, C), jnp.bfloat16),
        scratch_shapes=[
            pltpu.VMEM((4, K2, C), jnp.bfloat16),
            pltpu.VMEM((3, LAT_ROWS, W, LANES), jnp.bfloat16),
            pltpu.VMEM((3, LAT_ROWS, W, LANES), jnp.bfloat16),
            pltpu.VMEM((ACT_FRAMES, ACT_ROWS, WIDE, C), jnp.bfloat16),
            pltpu.VMEM((4, ACT_ROWS, WIDE, C), jnp.bfloat16),
            pltpu.VMEM((3, SLAB + 8, LANES), jnp.float32),
            pltpu.VMEM((FCAP, SLAB, C), jnp.bfloat16),
            pltpu.SemaphoreType.DMA((4,)),
            pltpu.SemaphoreType.DMA((FCAP,)),
        ],
        compiler_params=pltpu.CompilerParams(vmem_limit_bytes=50 * 1024 * 1024),
        name="two_convs",
    )(counts, got, w1, b1, b2, mid, mix)


def frame_pair_kernel(in_kernel):
    taps = jnp.transpose(in_kernel, (1, 2, 0, 3, 4)).reshape(3, 3, 3 * Z, C)
    even = jnp.pad(taps, ((0, 0), (0, 0), (0, Z), (0, 0)))
    odd = jnp.pad(taps, ((0, 0), (0, 0), (Z, 0), (0, 0)))
    both = jnp.concatenate([even, odd], axis=-1)
    return jnp.concatenate(
        [both[:, :2].reshape(384, 2 * C), both[:, 2].reshape(192, 2 * C),
         jnp.zeros((64, 2 * C), in_kernel.dtype)], axis=0)


def mix_kernel(mid_hbm, out_hbm, mids, mixes, in_sems, out_sems):
    block = K2 // MIX_STEPS

    def rows_of(k):
        return pl.ds(pl.multiple_of(k * block, block), block)

    def pull(k):
        return pltpu.make_async_copy(mid_hbm.at[:, rows_of(k)], mids.at[:, rows_of(k)], in_sems.at[k])

    def push(k):
        return pltpu.make_async_copy(mixes.at[:, rows_of(k)], out_hbm.at[:, rows_of(k)], out_sems.at[k])

    for k in range(MIX_STEPS):
        pull(k).start()

    def step(k, carry):
        pull(k).wait()
        ends = mids[0, rows_of(k)].astype(jnp.float32) + mids[2, rows_of(k)].astype(jnp.float32)
        middle = mids[1, rows_of(k)].astype(jnp.float32)
        mixes[0, rows_of(k)] = (ends + middle).astype(jnp.bfloat16)
        mixes[1, rows_of(k)] = (ends - middle).astype(jnp.bfloat16)
        push(k).start()
        return carry

    lax.fori_loop(0, MIX_STEPS, step, 0)
    for k in range(MIX_STEPS):
        push(k).wait()


def time_mixes(mid):
    return pl.pallas_call(
        mix_kernel,
        in_specs=[pl.BlockSpec(memory_space=pl.ANY)],
        out_specs=pl.BlockSpec(memory_space=pl.ANY),
        out_shape=jax.ShapeDtypeStruct((2, K2, C), jnp.bfloat16),
        scratch_shapes=[
            pltpu.VMEM((3, K2, C), jnp.bfloat16),
            pltpu.VMEM((2, K2, C), jnp.bfloat16),
            pltpu.SemaphoreType.DMA((MIX_STEPS,)),
            pltpu.SemaphoreType.DMA((MIX_STEPS,)),
        ],
        compiler_params=pltpu.CompilerParams(vmem_limit_bytes=52 * 1024 * 1024),
        cost_estimate=pl.CostEstimate(
            flops=6 * K2 * C, bytes_accessed=10 * K2 * C, transcendentals=0),
        name="time_mixes",
    )(mid)


def per_device(latents, token_cell, frame_counts, in_kernel, in_bias, mid_kernel, mid_bias):
    windows = sort_tokens(frame_counts, token_cell, latents.T)
    by_band = lax.all_to_all(windows, "band", split_axis=0, concat_axis=0, tiled=True)
    by_band, w1 = lax.optimization_barrier((by_band, frame_pair_kernel(in_kernel)))
    pairs = by_band.reshape(ROWS, 2, SPAN, LANES)
    edge = jnp.zeros((1, 1, SPAN, LANES), by_band.dtype)
    above = jnp.concatenate([edge, pairs[:-1, 1:]], axis=0)
    below = jnp.concatenate([pairs[1:, :1], edge], axis=0)
    spread = jnp.concatenate([above, pairs, below], axis=1)
    spread, mid = lax.optimization_barrier((spread, mid_kernel.reshape(3, K2, C)))
    got = lax.all_to_all(spread, "rows", split_axis=0, concat_axis=0, tiled=True)
    out = convs(frame_counts, got, w1, in_bias, mid_bias, mid, time_mixes(mid))
    return out.reshape(FCAP, R, W, C)


def solution(mesh):
    placed = (P(("band", "rows"), None), P(("band", "rows")), P(), P(), P(), P(), P())
    return jax.shard_map(
        per_device,
        mesh=mesh,
        in_specs=placed,
        out_specs=P("band", "rows", None, None),
        check_vma=False,
    )
```
